32 devices in a mesh: strip: 2 (over x), az: 4 (over z), tile: 4 (over y, core).
Axes of the slice: x: 2, y: 2, z: 4, core: 2. Of those that a mesh axis runs over, the one named last changes fastest.
Arguments:
- raw_echo: float32 [2, 4096, 4096], P(None, ('strip', 'az', 'tile')), parts along dimension 1, may hold values from -6 to 6
- phase_scaling: float32 [1024, 4096], P(None, 'tile'), may hold values from -3.140625 to 3.140625
- phase_range: float32 [1024, 4096], P('tile'), may hold values from -3.140625 to 3.140625
- phase_azimuth: float32 [1024, 4096], P(None, 'tile'), may hold values from -3.140625 to 3.140625
Outputs:
- image: float32 [2, 4096, 4096], P(None, ('strip', 'az'), 'tile'), parts along dimension 1
The draws below stay inside these ranges and needn't reach their ends.
There are 2 independent parts, one for each index of `strip`. The reference program is written for one: setup_inputs(seed, part) draws one part's arguments, and reference() takes and returns one part's arrays. A program takes and returns all parts, laid end to end along the dimension named above; an argument that names none is the same for every part. Nothing has to cross between parts.
All inputs are finite; a program needn't handle non-finite values.
Results may differ from the reference program's by a relative error of at most 0.00007.
Values sent between devices are 32-bit elements; how exact they have to be, the bound alone decides.
A program may use at most 128 MiB of HBM per device.

```python
import jax
import jax.numpy as jnp
from jax import lax

RANGES = 4096
PULSES = 512
TAIL = 512
LENGTH = 1024
STRIP_PULSES = 2048
N_AZ = 4


def block_levels(stream_key, extent, cuts, low, top_value):
    def one(dim, blocks):
        steps = jax.random.uniform(jax.random.fold_in(jax.random.fold_in(stream_key, 6), dim), (blocks,), jnp.float32, low / len(cuts), top_value / len(cuts))
        return jnp.repeat(jnp.exp(steps), extent[dim] // blocks).reshape((-1,) + (1,) * (len(extent) - dim - 1))

    loudness = one(*cuts[0])
    for cut in cuts[1:]:
        loudness = loudness * one(*cut)
    return loudness


def gaussian(own_key, shape, scale, bound, shards=(), dtype=jnp.bfloat16):
    result = jax.random.normal(own_key, shape, jnp.float32) * scale
    if len(shards) > 0:
        result = block_levels(own_key, shape, shards, -0.22, 0.18) * result
    return jnp.clip(result, min=-bound, max=bound).astype(dtype)


def setup_inputs(seed: int = 0, part: int = 0) -> dict:
    key_list = jax.random.split(jax.random.key(seed), 5)
    own_keys = jax.random.split(jax.random.fold_in(key_list[4], part), 5)
    return {
        "raw_echo": gaussian(own_keys[0], (2, STRIP_PULSES, RANGES), 1.0, 6.0, ((1, 16),), jnp.float32),
        "phase_scaling": jnp.clip(jax.random.uniform(key_list[1], (LENGTH, RANGES), jnp.float32, -3.140625, 3.140625), -3.140625, 3.140625),
        "phase_range": jnp.clip(jax.random.uniform(key_list[2], (LENGTH, RANGES), jnp.float32, -3.140625, 3.140625), -3.140625, 3.140625),
        "phase_azimuth": jnp.clip(jax.random.uniform(key_list[3], (LENGTH, RANGES), jnp.float32, -3.140625, 3.140625), -3.140625, 3.140625),
    }


def reference(raw_echo, phase_scaling, phase_range, phase_azimuth):
    blocks = raw_echo.reshape(2, N_AZ, PULSES, RANGES).transpose(1, 0, 2, 3)
    turn_one = lax.complex(jnp.cos(phase_scaling), jnp.sin(phase_scaling))
    turn_two = lax.complex(jnp.cos(phase_range), jnp.sin(phase_range))
    turn_three = lax.complex(jnp.cos(phase_azimuth), jnp.sin(phase_azimuth))

    def focus_block(block):
        signal = lax.complex(block[0], block[1])
        signal = jnp.pad(signal, ((0, TAIL), (0, 0)))
        signal = jnp.fft.fft(signal, axis=0) * turn_one
        signal = jnp.fft.fft(signal, axis=1) * turn_two
        signal = jnp.fft.ifft(signal, axis=1) * turn_three
        signal = jnp.fft.ifft(signal, axis=0)
        return jnp.stack([jnp.real(signal), jnp.imag(signal)])

    focused = lax.map(focus_block, blocks)
    head_rows = focused[:, :, :PULSES]
    tail_rows = focused[:, :, PULSES:]
    previous = jnp.concatenate([jnp.zeros_like(tail_rows[:1]), tail_rows[:-1]], axis=0)
    head_rows = head_rows.at[:, :, :TAIL].add(previous)
    return head_rows.transpose(1, 0, 2, 3).reshape(2, N_AZ * PULSES, RANGES)
```

```python
import functools
import math

import jax
import jax.numpy as jnp
import numpy as np
from jax import lax
from jax.experimental import pallas as pl
from jax.experimental.pallas import tpu as pltpu
from jax.sharding import PartitionSpec as P

F32 = jnp.float32
BF16 = jnp.bfloat16
LANES = 128


def halves(table):
    hi = np.asarray(table, np.float32).astype(jnp.bfloat16)
    lo = (np.asarray(table, np.float64) - hi.astype(np.float64)).astype(jnp.bfloat16)
    return np.stack([hi, lo])


def roots(rows, cols, modulus, direction):
    residue = np.outer(rows, cols) % modulus
    angle = residue * (direction * 2.0 * math.pi / modulus)
    return np.cos(angle), np.sin(angle)


def left_table(rows, cols, modulus, direction, scale=1.0):
    c, s = roots(rows, cols, modulus, direction)
    return halves(np.block([[c, -s], [s, c]]) * scale)


def right_table(rows, cols, modulus, direction, scale=1.0):
    c, s = roots(rows, cols, modulus, direction)
    return halves(np.block([[c, s], [-s, c]]) * scale)


def twist_table(count, length, modulus, direction):
    c, s = roots(np.arange(count), np.arange(length), modulus, direction)
    full = np.stack([c, s]).astype(np.float32)
    return np.ascontiguousarray(np.broadcast_to(full[..., None], full.shape + (LANES,)))


def split(x):
    hi = x.astype(BF16)
    return hi, (x - hi.astype(F32)).astype(BF16)


def mm(a, b):
    return jnp.dot(a, b, preferred_element_type=F32)


def times(a, t):
    return a[0] * t[0] - a[1] * t[1], a[0] * t[1] + a[1] * t[0]


def plus(a, b):
    return a[0] + b[0], a[1] + b[1]


def minus(a, b):
    return a[0] - b[0], a[1] - b[1]


def quarter(a, direction):
    return (-a[1], a[0]) if direction > 0 else (a[1], -a[0])


def four(v, direction):
    a, b = plus(v[0], v[2]), minus(v[0], v[2])
    c, d = plus(v[1], v[3]), quarter(minus(v[1], v[3]), direction)
    return [plus(a, c), plus(b, d), minus(a, c), minus(b, d)]


def fft(v, direction):
    n = len(v)
    if n == 1:
        return v
    if n == 2:
        return [plus(v[0], v[1]), minus(v[0], v[1])]
    if n == 4:
        return four(v, direction)
    parts = [fft(v[e::4], direction) for e in range(4)] if n % 4 == 0 else None
    out = [None] * n
    m = n // 4
    for f in range(m):
        items = []
        for e in range(4):
            x = parts[e][f]
            k = e * f % n
            if k == 0:
                pass
            elif 8 * k == n:
                h = np.float32(math.sqrt(0.5))
                q = quarter(x, direction)
                x = ((x[0] + q[0]) * h, (x[1] + q[1]) * h)
            elif 4 * k == n:
                x = quarter(x, direction)
            elif 8 * k == 3 * n:
                h = np.float32(math.sqrt(0.5))
                q = quarter(x, direction)
                x = ((q[0] - x[0]) * h, (q[1] - x[1]) * h)
            else:
                ang = direction * 2.0 * math.pi * k / n
                x = times(x, (np.float32(math.cos(ang)), np.float32(math.sin(ang))))
            items.append(x)
        got = four(items, direction)
        for j in range(4):
            out[f + j * m] = got[j]
    return out


def front_kernel(x_ref, table_ref, twist_ref, cos_ref, sin_ref, o_ref):
    q = x_ref.shape[1] // 4
    m = o_ref.shape[1] // 4
    width = x_ref.shape[2]
    hi, lo = table_ref[0], table_ref[1]
    z = []
    for e in range(4):
        rows = pl.ds(e, q, stride=4)
        s = jnp.concatenate([x_ref[0, rows, :], x_ref[1, rows, :]], axis=0)
        s_hi, s_lo = split(s)
        r = mm(hi, s_hi) + mm(hi, s_lo) + mm(lo, s_hi)
        r = (r[:m], r[m:])
        if e:
            r = times(r, (twist_ref[0, e], twist_ref[1, e]))
        z.append(r)
    for j, x in enumerate(four(z, -1)):
        rows = pl.ds(j * m, m)
        x = times(x, (cos_ref[rows, :], sin_ref[rows, :]))
        o_ref[0, rows, :] = x[0]
        o_ref[1, rows, :] = x[1]


def back_kernel(x_ref, table_ref, twist_ref, cos_ref, sin_ref, o_ref):
    m = x_ref.shape[1] // 4
    q = o_ref.shape[1] // 4
    hi, lo = table_ref[0], table_ref[1]
    v = []
    for j in range(4):
        rows = pl.ds(j * m, m)
        v.append(times((x_ref[0, rows, :], x_ref[1, rows, :]), (cos_ref[rows, :], sin_ref[rows, :])))
    for e, x in enumerate(four(v, 1)):
        if e:
            x = times(x, (twist_ref[0, e], twist_ref[1, e]))
        s_hi, s_lo = split(jnp.concatenate(x, axis=0))
        r = mm(hi, s_hi) + mm(hi, s_lo) + mm(lo, s_hi)
        rows = pl.ds(e, q, stride=4)
        o_ref[0, rows, :] = r[:q]
        o_ref[1, rows, :] = r[q:]


def range_kernel(x_ref, fwd_ref, inv_ref, twist_ref, cos_ref, sin_ref, o_ref, hi_ref, lo_ref, mid_ref):
    block = x_ref.shape[1]
    n_one = cos_ref.shape[0]
    step = 16
    f_hi, f_lo = fwd_ref[0], fwd_ref[1]
    b_hi, b_lo = inv_ref[0], inv_ref[1]

    @pl.loop(0, block // step)
    def _(i):
        rows = pl.ds(pl.multiple_of(i * step, step), step)
        v = [
            tuple(x_ref[c, rows, pl.ds(a * LANES, LANES)] for c in (0, 1))
            for a in range(n_one)
        ]
        for k, x in enumerate(fft(v, -1)):
            if k:
                x = times(x, (twist_ref[0, k : k + 1, :], twist_ref[1, k : k + 1, :]))
            for c in (0, 1):
                h, l = split(x[c])
                hi_ref[k, rows, pl.ds(c * LANES, LANES)] = h
                lo_ref[k, rows, pl.ds(c * LANES, LANES)] = l

    group = 4

    @pl.loop(0, n_one // group)
    def _(i):
        ks = pl.ds(i * group, group)
        flat = (group * block, 2 * LANES)
        h, l = hi_ref[ks].reshape(flat), lo_ref[ks].reshape(flat)
        r = mm(h, f_hi) + mm(l, f_hi) + mm(h, f_lo)
        c = cos_ref[ks].reshape(group * block, LANES)
        s = sin_ref[ks].reshape(group * block, LANES)
        r = times((r[:, :LANES], r[:, LANES:]), (c, s))
        h, l = split(jnp.concatenate(r, axis=1))
        r = mm(h, b_hi) + mm(l, b_hi) + mm(h, b_lo)
        mid_ref[ks] = r.reshape(group, block, 2 * LANES)

    @pl.loop(0, block // 8)
    def _(i):
        rows = pl.ds(pl.multiple_of(i * 8, 8), 8)
        v = []
        for k in range(n_one):
            x = tuple(mid_ref[k, rows, pl.ds(c * LANES, LANES)] for c in (0, 1))
            if k:
                x = times(x, (twist_ref[0, k : k + 1, :], -twist_ref[1, k : k + 1, :]))
            v.append(x)
        for a, x in enumerate(fft(v, 1)):
            for c in (0, 1):
                o_ref[c, rows, pl.ds(a * LANES, LANES)] = x[c]


def azimuth(kernel, x, table, twist, cos, sin, rows):
    width = x.shape[2]
    tile = LANES
    whole = lambda a: pl.BlockSpec(a.shape, lambda i: (0,) * a.ndim)
    return pl.pallas_call(
        kernel,
        grid=(width // tile,),
        out_shape=jax.ShapeDtypeStruct((2, rows, width), F32),
        in_specs=[
            pl.BlockSpec((2, x.shape[1], tile), lambda i: (0, 0, i)),
            whole(table),
            whole(twist),
            pl.BlockSpec((cos.shape[0], tile), lambda i: (0, i)),
            pl.BlockSpec((cos.shape[0], tile), lambda i: (0, i)),
        ],
        out_specs=pl.BlockSpec((2, rows, tile), lambda i: (0, 0, i)),
        compiler_params=pltpu.CompilerParams(vmem_limit_bytes=48 << 20),
        cost_estimate=pl.CostEstimate(
            flops=6 * table.shape[1] * table.shape[2] * 4 * width,
            bytes_accessed=4 * (x.size + 2 * cos.size + 2 * rows * width),
            transcendentals=0,
        ),
    )(x, table, twist, cos, sin)


def range_filter(x, fwd, inv, twist, cos, sin):
    _, count, extent = x.shape
    n_one = extent // LANES
    block = min(64, count)
    whole = lambda a: pl.BlockSpec(a.shape, lambda i: (0,) * a.ndim)
    return pl.pallas_call(
        range_kernel,
        grid=(count // block,),
        out_shape=jax.ShapeDtypeStruct(x.shape, F32),
        in_specs=[
            pl.BlockSpec((2, block, extent), lambda i: (0, i, 0)),
            whole(fwd),
            whole(inv),
            whole(twist),
            pl.BlockSpec((n_one, block, LANES), lambda i: (0, i, 0)),
            pl.BlockSpec((n_one, block, LANES), lambda i: (0, i, 0)),
        ],
        out_specs=pl.BlockSpec((2, block, extent), lambda i: (0, i, 0)),
        scratch_shapes=[
            pltpu.VMEM((n_one, block, 2 * LANES), BF16),
            pltpu.VMEM((n_one, block, 2 * LANES), BF16),
            pltpu.VMEM((n_one, block, 2 * LANES), F32),
        ],
        compiler_params=pltpu.CompilerParams(vmem_limit_bytes=48 << 20),
        cost_estimate=pl.CostEstimate(
            flops=12 * x.size * 256, bytes_accessed=4 * 3 * x.size, transcendentals=0
        ),
    )(x, fwd, inv, twist, cos, sin)


def body(raw_echo, phase_scaling, phase_range, phase_azimuth):
    tiles = lax.axis_size("tile")
    columns = lax.all_to_all(raw_echo, "tile", split_axis=2, concat_axis=1, tiled=True)
    pulses, width = columns.shape[1:]
    extent = phase_scaling.shape[0]
    m, q = extent // 4, pulses // 4
    count, ranges = phase_range.shape
    n_one = ranges // LANES
    rows = np.arange(m)
    table = left_table(rows, np.arange(q), m, -1)
    spectrum = azimuth(
        front_kernel, columns, table, twist_table(4, m, extent, -1),
        jnp.cos(phase_scaling), jnp.sin(phase_scaling), extent,
    )
    grouped = spectrum.reshape(2, tiles, extent // tiles, width)
    doppler = lax.all_to_all(grouped, "tile", split_axis=1, concat_axis=3, tiled=True)
    permuted = phase_range.reshape(count, LANES, n_one).transpose(2, 0, 1)
    lane = np.arange(LANES)
    c, s = roots(np.arange(n_one), lane, ranges, -1)
    filtered = range_filter(
        doppler.reshape(2, count, ranges),
        right_table(lane, lane, LANES, -1),
        right_table(lane, lane, LANES, 1, 1.0 / ranges),
        np.stack([c, s]).astype(np.float32),
        jnp.cos(permuted), jnp.sin(permuted),
    )
    returned = lax.all_to_all(filtered[:, None], "tile", split_axis=3, concat_axis=1, tiled=True)
    returned = returned.reshape(2, extent, width)
    twist = twist_table(4, m, extent, 1)
    cos, sin = jnp.cos(phase_azimuth), jnp.sin(phase_azimuth)
    rest = azimuth(
        back_kernel, returned, left_table(rows[q:], rows, m, 1, 1.0 / extent), twist,
        cos, sin, extent - pulses,
    )
    length = lax.axis_size("az")
    incoming = lax.ppermute(rest, "az", [(i, i + 1) for i in range(length - 1)])
    head = azimuth(
        back_kernel, returned, left_table(rows[:q], rows, m, 1, 1.0 / extent), twist,
        cos, sin, pulses,
    )
    tail = extent - pulses
    if tail == pulses:
        return head + incoming
    return jnp.concatenate([head[:, :tail] + incoming, head[:, tail:]], axis=1)


def solution(mesh):
    return jax.shard_map(
        body,
        mesh=mesh,
        in_specs=(
            P(None, ("strip", "az", "tile"), None),
            P(None, "tile"),
            P("tile", None),
            P(None, "tile"),
        ),
        out_specs=P(None, ("strip", "az"), "tile"),
        check_vma=False,
    )
```

```python
import functools
import math

import jax
import jax.numpy as jnp
import numpy as np
from jax import lax
from jax.experimental import pallas as pl
from jax.experimental.pallas import tpu as pltpu
from jax.sharding import PartitionSpec as P

F32 = jnp.float32
BF16 = jnp.bfloat16
LANES = 128


def halves(table):
    hi = np.asarray(table, np.float32).astype(jnp.bfloat16)
    lo = (np.asarray(table, np.float64) - hi.astype(np.float64)).astype(jnp.bfloat16)
    return np.stack([hi, lo])


def roots(rows, cols, modulus, direction):
    residue = np.outer(rows, cols) % modulus
    angle = residue * (direction * 2.0 * math.pi / modulus)
    return np.cos(angle), np.sin(angle)


def left_table(rows, cols, modulus, direction, scale=1.0):
    c, s = roots(rows, cols, modulus, direction)
    return halves(np.block([[c, -s], [s, c]]) * scale)


def right_table(rows, cols, modulus, direction, scale=1.0):
    c, s = roots(rows, cols, modulus, direction)
    return halves(np.block([[c, s], [-s, c]]) * scale)


def twist_table(count, length, modulus, direction):
    c, s = roots(np.arange(count), np.arange(length), modulus, direction)
    full = np.stack([c, s]).astype(np.float32)
    return np.ascontiguousarray(np.broadcast_to(full[..., None], full.shape + (LANES,)))


def split(x):
    hi = x.astype(BF16)
    return hi, (x - hi.astype(F32)).astype(BF16)


def mm(a, b):
    return jnp.dot(a, b, preferred_element_type=F32)


def times(a, t):
    return a[0] * t[0] - a[1] * t[1], a[0] * t[1] + a[1] * t[0]


def plus(a, b):
    return a[0] + b[0], a[1] + b[1]


def minus(a, b):
    return a[0] - b[0], a[1] - b[1]


def quarter(a, direction):
    return (-a[1], a[0]) if direction > 0 else (a[1], -a[0])


def four(v, direction):
    a, b = plus(v[0], v[2]), minus(v[0], v[2])
    c, d = plus(v[1], v[3]), quarter(minus(v[1], v[3]), direction)
    return [plus(a, c), plus(b, d), minus(a, c), minus(b, d)]


def fft(v, direction):
    n = len(v)
    if n == 1:
        return v
    if n == 2:
        return [plus(v[0], v[1]), minus(v[0], v[1])]
    if n == 4:
        return four(v, direction)
    parts = [fft(v[e::4], direction) for e in range(4)] if n % 4 == 0 else None
    out = [None] * n
    m = n // 4
    for f in range(m):
        items = []
        for e in range(4):
            x = parts[e][f]
            k = e * f % n
            if k == 0:
                pass
            elif 8 * k == n:
                h = np.float32(math.sqrt(0.5))
                q = quarter(x, direction)
                x = ((x[0] + q[0]) * h, (x[1] + q[1]) * h)
            elif 4 * k == n:
                x = quarter(x, direction)
            elif 8 * k == 3 * n:
                h = np.float32(math.sqrt(0.5))
                q = quarter(x, direction)
                x = ((q[0] - x[0]) * h, (q[1] - x[1]) * h)
            else:
                ang = direction * 2.0 * math.pi * k / n
                x = times(x, (np.float32(math.cos(ang)), np.float32(math.sin(ang))))
            items.append(x)
        got = four(items, direction)
        for j in range(4):
            out[f + j * m] = got[j]
    return out


def sincos(x):
    y = x * 0.5
    z = y * y
    s, c = -1.0 / 39916800, 1.0 / 479001600
    for a, b in ((362880, -3628800), (-5040, 40320), (120, -720), (-6, 24), (1, -2)):
        s = s * z + np.float32(1.0 / a)
        c = c * z + np.float32(1.0 / b)
    s = s * y
    c = c * z + 1.0
    return 1.0 - 2.0 * s * s, 2.0 * s * c


def greet(partners):
    barrier = pltpu.get_barrier_semaphore()
    for device in partners:
        pl.semaphore_signal(barrier, inc=1, device_id=device, device_id_type=pl.DeviceIdType.MESH)
    return barrier


def lanes(j):
    return pl.ds(pl.multiple_of(j * LANES, LANES), LANES)


def front_kernel(tiles, raw_ref, table_ref, twist_ref, phase_ref, o_ref, cols, send, recv, local):
    me = lax.axis_index("tile")
    rows_own = raw_ref.shape[1]
    m = o_ref.shape[1] // 4
    width = o_ref.shape[2]
    count = width // LANES
    own = pl.ds(pl.multiple_of(me * rows_own, rows_own), rows_own)

    def out(j, k):
        to = lax.rem(me + k, tiles)
        return pltpu.make_async_remote_copy(
            src_ref=raw_ref.at[:, :, lanes(to * count + j)],
            dst_ref=cols.at[j, :, own, :],
            send_sem=send.at[j, k - 1],
            recv_sem=recv.at[j, k - 1],
            device_id={"tile": to},
            device_id_type=pl.DeviceIdType.MESH,
        )

    def keep(j):
        return pltpu.make_async_copy(
            raw_ref.at[:, :, lanes(me * count + j)], cols.at[j, :, own, :], local.at[j]
        )

    barrier = greet([{"tile": lax.rem(me + k, tiles)} for k in range(1, tiles)])
    pl.semaphore_wait(barrier, tiles - 1)

    @pl.loop(0, count)
    def _(j):
        for k in range(1, tiles):
            out(j, k).start()
        keep(j).start()

    @pl.loop(0, count)
    def _(j):
        for k in range(1, tiles):
            out(j, k).wait_recv()
        keep(j).wait()
        hi, lo = table_ref[0], table_ref[1]
        q = cols.shape[2] // 4
        z = []
        for e in range(4):
            rows = pl.ds(e, q, stride=4)
            s = jnp.concatenate([cols[j, 0, rows, :], cols[j, 1, rows, :]], axis=0)
            s_hi, s_lo = split(s)
            r = mm(hi, s_hi) + mm(hi, s_lo) + mm(lo, s_hi)
            r = (r[:m], r[m:])
            if e:
                r = times(r, (twist_ref[0, e], twist_ref[1, e]))
            z.append(r)
        for f, x in enumerate(four(z, -1)):
            rows = pl.ds(f * m, m)
            x = times(x, sincos(phase_ref[rows, lanes(j)]))
            o_ref[0, rows, lanes(j)] = x[0]
            o_ref[1, rows, lanes(j)] = x[1]

    @pl.loop(0, count)
    def _(j):
        for k in range(1, tiles):
            out(j, k).wait_send()


def filter_rows(x_ref, base, block, fwd_ref, inv_ref, twist_ref, phase_ref, hi_ref, lo_ref, mid_ref):
    n_one = phase_ref.shape[0]
    step = 16
    f_hi, f_lo = fwd_ref[0], fwd_ref[1]
    b_hi, b_lo = inv_ref[0], inv_ref[1]

    @pl.loop(0, block // step)
    def _(i):
        rows = pl.ds(pl.multiple_of(i * step, step), step)
        at = pl.ds(pl.multiple_of(base + i * step, step), step)
        v = [
            tuple(x_ref[c, at, pl.ds(a * LANES, LANES)] for c in (0, 1))
            for a in range(n_one)
        ]
        for k, x in enumerate(fft(v, -1)):
            if k:
                x = times(x, (twist_ref[0, k : k + 1, :], twist_ref[1, k : k + 1, :]))
            for c in (0, 1):
                h, l = split(x[c])
                hi_ref[k, rows, pl.ds(c * LANES, LANES)] = h
                lo_ref[k, rows, pl.ds(c * LANES, LANES)] = l

    group = 4

    @pl.loop(0, n_one // group)
    def _(i):
        ks = pl.ds(i * group, group)
        flat = (group * block, 2 * LANES)
        h, l = hi_ref[ks].reshape(flat), lo_ref[ks].reshape(flat)
        r = mm(h, f_hi) + mm(l, f_hi) + mm(h, f_lo)
        turn = phase_ref[ks, pl.ds(pl.multiple_of(base, block), block), :]
        r = times((r[:, :LANES], r[:, LANES:]), sincos(turn.reshape(group * block, LANES)))
        h, l = split(jnp.concatenate(r, axis=1))
        r = mm(h, b_hi) + mm(l, b_hi) + mm(h, b_lo)
        mid_ref[ks] = r.reshape(group, block, 2 * LANES)

    @pl.loop(0, block // 8)
    def _(i):
        rows = pl.ds(pl.multiple_of(i * 8, 8), 8)
        at = pl.ds(pl.multiple_of(base + i * 8, 8), 8)
        v = []
        for k in range(n_one):
            x = tuple(mid_ref[k, rows, pl.ds(c * LANES, LANES)] for c in (0, 1))
            if k:
                x = times(x, (twist_ref[0, k : k + 1, :], -twist_ref[1, k : k + 1, :]))
            v.append(x)
        for a, x in enumerate(fft(v, 1)):
            for c in (0, 1):
                x_ref[c, at, pl.ds(a * LANES, LANES)] = x[c]


def back_kernel(
    tiles, length, block,
    spec_ref, turn_ref, phase_ref, fwd_ref, inv_ref, range_twist_ref, table_ref, twist_ref,
    o_ref,
    dop, ret, tail_out, tail_in, head, hi_ref, lo_ref, mid_ref,
    send_a, recv_a, local_a, send_b, recv_b, local_b, send_c, recv_c,
):
    me = lax.axis_index("tile")
    az = lax.axis_index("az")
    count = dop.shape[1]
    width = o_ref.shape[2]
    pulses = o_ref.shape[1]
    tail = tail_out.shape[2]
    blocks = count // block
    spans = width // LANES
    mine = pl.ds(pl.multiple_of(me * width, LANES), width)
    own = pl.ds(pl.multiple_of(me * count, count), count)

    def out(i, k):
        to = lax.rem(me + k, tiles)
        return pltpu.make_async_remote_copy(
            src_ref=spec_ref.at[:, pl.ds(pl.multiple_of(to * count + i * block, block), block), :],
            dst_ref=dop.at[:, pl.ds(pl.multiple_of(i * block, block), block), mine],
            send_sem=send_a.at[i, k - 1],
            recv_sem=recv_a.at[i, k - 1],
            device_id={"tile": to},
            device_id_type=pl.DeviceIdType.MESH,
        )

    def back(j, k):
        to = lax.rem(me + k, tiles)
        return pltpu.make_async_remote_copy(
            src_ref=dop.at[:, :, lanes(to * spans + j)],
            dst_ref=ret.at[j, :, own, :],
            send_sem=send_b.at[j, k - 1],
            recv_sem=recv_b.at[j, k - 1],
            device_id={"tile": to},
            device_id_type=pl.DeviceIdType.MESH,
        )

    def keep(j):
        return pltpu.make_async_copy(
            dop.at[:, :, lanes(me * spans + j)], ret.at[j, :, own, :], local_b.at[j]
        )

    def onward(j):
        return pltpu.make_async_remote_copy(
            src_ref=tail_out.at[j],
            dst_ref=tail_in.at[j],
            send_sem=send_c.at[j],
            recv_sem=recv_c.at[j],
            device_id={"az": lax.rem(az + 1, length)},
            device_id_type=pl.DeviceIdType.MESH,
        )

    barrier = greet(
        [{"tile": lax.rem(me + k, tiles)} for k in range(1, tiles)]
        + [{"az": lax.rem(az + 1, length)}, {"az": lax.rem(az + length - 1, length)}]
    )
    pl.semaphore_wait(barrier, tiles + 1)

    @pl.loop(0, blocks)
    def _(i):
        for k in range(1, tiles):
            out(i, k).start()

    first = pltpu.make_async_copy(spec_ref.at[:, own, :], dop.at[:, :, mine], local_a)
    first.start()
    first.wait()

    @pl.loop(0, blocks)
    def _(i):
        for k in range(1, tiles):
            out(i, k).wait_recv()
        filter_rows(
            dop, i * block, block, fwd_ref, inv_ref, range_twist_ref, turn_ref,
            hi_ref, lo_ref, mid_ref,
        )

    @pl.loop(0, spans)
    def _(j):
        for k in range(1, tiles):
            back(j, k).start()
        keep(j).start()

    @pl.loop(0, spans)
    def _(j):
        for k in range(1, tiles):
            back(j, k).wait_recv()
        keep(j).wait()
        m = ret.shape[2] // 4
        q = pulses // 4
        hi, lo = table_ref[0], table_ref[1]
        v = []
        for f in range(4):
            rows = pl.ds(f * m, m)
            v.append(times((ret[j, 0, rows, :], ret[j, 1, rows, :]), sincos(phase_ref[rows, lanes(j)])))
        for e, x in enumerate(four(v, 1)):
            if e:
                x = times(x, (twist_ref[0, e], twist_ref[1, e]))
            s_hi, s_lo = split(jnp.concatenate(x, axis=0))
            r = mm(hi, s_hi) + mm(hi, s_lo) + mm(lo, s_hi)
            for c in (0, 1):
                head[c, pl.ds(e, q, stride=4), :] = r[c * m : c * m + q]
                tail_out[j, c, pl.ds(e, m - q, stride=4), :] = r[c * m + q : (c + 1) * m]

        @pl.when(az < length - 1)
        def _():
            onward(j).start()

        o_ref[:, :, lanes(j)] = head[...]

    @pl.when(az > 0)
    def _():
        @pl.loop(0, spans)
        def _(j):
            onward(j).wait_recv()
            o_ref[:, pl.ds(0, tail), lanes(j)] += tail_in[j]

    @pl.loop(0, blocks)
    def _(i):
        for k in range(1, tiles):
            out(i, k).wait_send()

    @pl.loop(0, spans)
    def _(j):
        for k in range(1, tiles):
            back(j, k).wait_send()

    @pl.when(az < length - 1)
    def _():
        @pl.loop(0, spans)
        def _(j):
            onward(j).wait_send()


def body(raw_echo, phase_scaling, phase_range, phase_azimuth):
    tiles = lax.axis_size("tile")
    length = lax.axis_size("az")
    rows_own = raw_echo.shape[1]
    pulses = rows_own * tiles
    extent, width = phase_scaling.shape
    count, ranges = phase_range.shape
    m, q, tail = extent // 4, pulses // 4, extent - pulses
    n_one, spans = ranges // LANES, width // LANES
    block = min(64, count)
    rows, lane = np.arange(m), np.arange(LANES)
    vmem = pl.BlockSpec(memory_space=pltpu.VMEM)
    anyspace = pl.BlockSpec(memory_space=pl.ANY)
    dma = pltpu.SemaphoreType.DMA
    spectrum = pl.pallas_call(
        functools.partial(front_kernel, tiles),
        out_shape=jax.ShapeDtypeStruct((2, extent, width), F32),
        in_specs=[anyspace, vmem, vmem, vmem],
        out_specs=vmem,
        scratch_shapes=[
            pltpu.VMEM((spans, 2, pulses, LANES), F32),
            dma((spans, tiles - 1)),
            dma((spans, tiles - 1)),
            dma((spans,)),
        ],
        compiler_params=pltpu.CompilerParams(
            collective_id=0, has_side_effects=True, vmem_limit_bytes=60 << 20
        ),
    )(
        raw_echo,
        left_table(rows, np.arange(q), m, -1),
        twist_table(4, m, extent, -1),
        phase_scaling,
    )
    turn = phase_range.reshape(count, LANES, n_one).transpose(2, 0, 1)
    c, s = roots(np.arange(n_one), lane, ranges, -1)
    return pl.pallas_call(
        functools.partial(back_kernel, tiles, length, block),
        out_shape=jax.ShapeDtypeStruct((2, pulses, width), F32),
        in_specs=[anyspace] + [vmem] * 7,
        out_specs=vmem,
        scratch_shapes=[
            pltpu.VMEM((2, count, ranges), F32),
            pltpu.VMEM((spans, 2, extent, LANES), F32),
            pltpu.VMEM((spans, 2, tail, LANES), F32),
            pltpu.VMEM((spans, 2, tail, LANES), F32),
            pltpu.VMEM((2, pulses, LANES), F32),
            pltpu.VMEM((n_one, block, 2 * LANES), BF16),
            pltpu.VMEM((n_one, block, 2 * LANES), BF16),
            pltpu.VMEM((n_one, block, 2 * LANES), F32),
            dma((count // block, tiles - 1)),
            dma((count // block, tiles - 1)),
            dma,
            dma((spans, tiles - 1)),
            dma((spans, tiles - 1)),
            dma((spans,)),
            dma((spans,)),
            dma((spans,)),
        ],
        compiler_params=pltpu.CompilerParams(
            collective_id=1, has_side_effects=True, vmem_limit_bytes=60 << 20
        ),
    )(
        spectrum,
        turn,
        phase_azimuth,
        right_table(lane, lane, LANES, -1),
        right_table(lane, lane, LANES, 1, 1.0 / ranges),
        np.stack([c, s]).astype(np.float32),
        left_table(rows, rows, m, 1, 1.0 / extent),
        twist_table(4, m, extent, 1),
    )


def solution(mesh):
    return jax.shard_map(
        body,
        mesh=mesh,
        in_specs=(
            P(None, ("strip", "az", "tile"), None),
            P(None, "tile"),
            P("tile", None),
            P(None, "tile"),
        ),
        out_specs=P(None, ("strip", "az"), "tile"),
        check_vma=False,
    )
```

```python
import functools
import math

import jax
import jax.numpy as jnp
import numpy as np
from jax import lax
from jax.experimental import pallas as pl
from jax.experimental.pallas import tpu as pltpu
from jax.sharding import PartitionSpec as P

F32 = jnp.float32
BF16 = jnp.bfloat16
LANES = 128


def halves(table):
    hi = np.asarray(table, np.float32).astype(jnp.bfloat16)
    lo = (np.asarray(table, np.float64) - hi.astype(np.float64)).astype(jnp.bfloat16)
    return np.stack([hi, lo])


def roots(rows, cols, modulus, direction):
    residue = np.outer(rows, cols) % modulus
    angle = residue * (direction * 2.0 * math.pi / modulus)
    return np.cos(angle), np.sin(angle)


def left_table(rows, cols, modulus, direction, scale=1.0):
    c, s = roots(rows, cols, modulus, direction)
    return halves(np.block([[c, -s], [s, c]]) * scale)


def right_table(rows, cols, modulus, direction, scale=1.0):
    c, s = roots(rows, cols, modulus, direction)
    return halves(np.block([[c, s], [-s, c]]) * scale)


def twist_table(count, length, modulus, direction):
    c, s = roots(np.arange(count), np.arange(length), modulus, direction)
    full = np.stack([c, s]).astype(np.float32)
    return np.ascontiguousarray(np.broadcast_to(full[..., None], full.shape + (LANES,)))


def split(x):
    hi = x.astype(BF16)
    return hi, (x - hi.astype(F32)).astype(BF16)


def mm(a, b):
    return jnp.dot(a, b, preferred_element_type=F32)


def times(a, t):
    return a[0] * t[0] - a[1] * t[1], a[0] * t[1] + a[1] * t[0]


def plus(a, b):
    return a[0] + b[0], a[1] + b[1]


def minus(a, b):
    return a[0] - b[0], a[1] - b[1]


def quarter(a, direction):
    return (-a[1], a[0]) if direction > 0 else (a[1], -a[0])


def four(v, direction):
    a, b = plus(v[0], v[2]), minus(v[0], v[2])
    c, d = plus(v[1], v[3]), quarter(minus(v[1], v[3]), direction)
    return [plus(a, c), plus(b, d), minus(a, c), minus(b, d)]


def fft(v, direction):
    n = len(v)
    if n == 1:
        return v
    if n == 2:
        return [plus(v[0], v[1]), minus(v[0], v[1])]
    if n == 4:
        return four(v, direction)
    parts = [fft(v[e::4], direction) for e in range(4)] if n % 4 == 0 else None
    out = [None] * n
    m = n // 4
    for f in range(m):
        items = []
        for e in range(4):
            x = parts[e][f]
            k = e * f % n
            if k == 0:
                pass
            elif 8 * k == n:
                h = np.float32(math.sqrt(0.5))
                q = quarter(x, direction)
                x = ((x[0] + q[0]) * h, (x[1] + q[1]) * h)
            elif 4 * k == n:
                x = quarter(x, direction)
            elif 8 * k == 3 * n:
                h = np.float32(math.sqrt(0.5))
                q = quarter(x, direction)
                x = ((q[0] - x[0]) * h, (q[1] - x[1]) * h)
            else:
                ang = direction * 2.0 * math.pi * k / n
                x = times(x, (np.float32(math.cos(ang)), np.float32(math.sin(ang))))
            items.append(x)
        got = four(items, direction)
        for j in range(4):
            out[f + j * m] = got[j]
    return out


def sincos(x):
    y = x * 0.5
    z = y * y
    s, c = -1.0 / 39916800, 1.0 / 479001600
    for a, b in ((362880, -3628800), (-5040, 40320), (120, -720), (-6, 24), (1, -2)):
        s = s * z + np.float32(1.0 / a)
        c = c * z + np.float32(1.0 / b)
    s = s * y
    c = c * z + 1.0
    return 1.0 - 2.0 * s * s, 2.0 * s * c


def greet(partners):
    barrier = pltpu.get_barrier_semaphore()
    for device in partners:
        pl.semaphore_signal(barrier, inc=1, device_id=device, device_id_type=pl.DeviceIdType.MESH)
    return barrier


def lanes(j):
    return pl.ds(pl.multiple_of(j * LANES, LANES), LANES)


def filter_rows(x_ref, base, block, fwd_ref, inv_ref, twist_ref, phase_ref, hi_ref, lo_ref, mid_ref):
    n_one = phase_ref.shape[0]
    step = 16
    f_hi, f_lo = fwd_ref[0], fwd_ref[1]
    b_hi, b_lo = inv_ref[0], inv_ref[1]

    @pl.loop(0, block // step)
    def _(i):
        rows = pl.ds(pl.multiple_of(i * step, step), step)
        at = pl.ds(pl.multiple_of(base + i * step, step), step)
        v = [
            tuple(x_ref[c, at, pl.ds(a * LANES, LANES)] for c in (0, 1))
            for a in range(n_one)
        ]
        for k, x in enumerate(fft(v, -1)):
            if k:
                x = times(x, (twist_ref[0, k : k + 1, :], twist_ref[1, k : k + 1, :]))
            for c in (0, 1):
                h, l = split(x[c])
                hi_ref[k, rows, pl.ds(c * LANES, LANES)] = h
                lo_ref[k, rows, pl.ds(c * LANES, LANES)] = l

    group = 4

    @pl.loop(0, n_one // group)
    def _(i):
        ks = pl.ds(i * group, group)
        flat = (group * block, 2 * LANES)
        h, l = hi_ref[ks].reshape(flat), lo_ref[ks].reshape(flat)
        r = mm(h, f_hi) + mm(l, f_hi) + mm(h, f_lo)
        turn = phase_ref[ks, pl.ds(pl.multiple_of(base, block), block), :]
        r = times((r[:, :LANES], r[:, LANES:]), sincos(turn.reshape(group * block, LANES)))
        h, l = split(jnp.concatenate(r, axis=1))
        r = mm(h, b_hi) + mm(l, b_hi) + mm(h, b_lo)
        at = pl.ds(pl.multiple_of(i * group * block, block), group * block)
        mid_ref[0, at, :] = r[:, :LANES]
        mid_ref[1, at, :] = r[:, LANES:]

    @pl.loop(0, block // 8)
    def _(i):
        at = pl.ds(pl.multiple_of(base + i * 8, 8), 8)
        v = []
        for k in range(n_one):
            x = tuple(mid_ref[c, pl.ds(pl.multiple_of(k * block + i * 8, 8), 8), :] for c in (0, 1))
            if k:
                x = times(x, (twist_ref[0, k : k + 1, :], -twist_ref[1, k : k + 1, :]))
            v.append(x)
        for a, x in enumerate(fft(v, 1)):
            for c in (0, 1):
                x_ref[c, at, pl.ds(a * LANES, LANES)] = x[c]


def permute_turn(o_ref, mid, turn):
    n_one, count, _ = turn.shape
    half = mid.shape[1]
    some = min(count, LANES)
    part = half // n_one

    @pl.loop(0, count // some)
    def _(i):
        @pl.loop(0, n_one)
        def _(g):
            c, row, j = piece(g, count, o_ref)
            at = pl.ds(pl.multiple_of(row + i * some, some), some)
            x = o_ref[c, at, lanes(j)]
            if some < LANES:
                x = jnp.concatenate([x] * (LANES // some), axis=0)
            per = half // LANES
            mid[g // per, pl.ds(pl.multiple_of(g % per * LANES, LANES), LANES), :] = x.T

        @pl.loop(0, n_one)
        def _(k):
            rows = pl.ds(k, part, stride=n_one)
            x = jnp.concatenate([mid[h, rows, :] for h in range(LANES // part)], axis=0)
            at = pl.ds(pl.multiple_of(i * some, some), some)
            turn[k, at, :] = x.T[:some]


def piece(g, count, o_ref):
    across = o_ref.shape[2] // LANES
    down = o_ref.shape[1] // count
    return g // (across * down), g // across % down * count, g % across


def focus_kernel(
    tiles, length, block,
    raw_ref, scaling_ref, range_ref, azimuth_ref,
    front_ref, twist_ref, fwd_ref, inv_ref, range_twist_ref, table_ref,
    o_ref,
    spec, scaling, turn, phase, dop, ret, tail_out, tail_in, head, hi_ref, lo_ref, mid,
    send_e, recv_e, local_e, send_a, recv_a, local_a, send_b, recv_b, local_b,
    send_c, recv_c, load, load_range,
):
    me = lax.axis_index("tile")
    az = lax.axis_index("az")
    count = dop.shape[1]
    width = o_ref.shape[2]
    pulses = o_ref.shape[1]
    tail = tail_in.shape[2]
    rows_own = raw_ref.shape[1]
    n_one = turn.shape[0]
    blocks = count // block
    early = (blocks - 1) * block
    spans = width // LANES
    cols = tail_out
    m = spec.shape[1] // 4
    q = pulses // 4
    mine = pl.ds(pl.multiple_of(me * width, LANES), width)
    own = pl.ds(pl.multiple_of(me * count, count), count)
    own_pulses = pl.ds(pl.multiple_of(me * rows_own, rows_own), rows_own)

    def remote(src, dst, send, recv, device):
        return pltpu.make_async_remote_copy(
            src_ref=src, dst_ref=dst, send_sem=send, recv_sem=recv,
            device_id=device, device_id_type=pl.DeviceIdType.MESH,
        )

    def echo(j, k):
        to = lax.rem(me + k, tiles)
        return remote(
            raw_ref.at[:, :, lanes(to * spans + j)], cols.at[j, :, own_pulses, :],
            send_e.at[j, k - 1], recv_e.at[j, k - 1], {"tile": to},
        )

    def keep_echo(j):
        return pltpu.make_async_copy(
            raw_ref.at[:, :, lanes(me * spans + j)], cols.at[j, :, own_pulses, :], local_e.at[j]
        )

    def load_piece(g):
        c, row, j = piece(g, count, o_ref)
        return pltpu.make_async_copy(
            range_ref.at[:, lanes(g)],
            o_ref.at[c, pl.ds(pl.multiple_of(row, count), count), lanes(j)],
            load_range.at[g],
        )

    def out(i, k):
        to = lax.rem(me + k, tiles)
        return remote(
            spec.at[:, pl.ds(pl.multiple_of(to * count + i * block, block), block), :],
            dop.at[:, pl.ds(pl.multiple_of(i * block, block), block), mine],
            send_a.at[i, k - 1], recv_a.at[i, k - 1], {"tile": to},
        )

    def back_rows(j, k, lo, n, slot):
        to = lax.rem(me + k, tiles)
        return remote(
            dop.at[:, pl.ds(lo, n), lanes(to * spans + j)],
            ret.at[j, :, pl.ds(pl.multiple_of(me * count + lo, 8), n), :],
            send_b.at[slot, k - 1], recv_b.at[slot, k - 1], {"tile": to},
        )

    def first_rows(k):
        return back_rows(0, k, 0, early, spans)

    def last_rows(k):
        return back_rows(0, k, early, count - early, 0)

    def back(j, k):
        return back_rows(j, k, 0, count, j)

    def keep(j):
        return pltpu.make_async_copy(
            dop.at[:, :, lanes(me * spans + j)], ret.at[j, :, own, :], local_b.at[j]
        )

    def onward(j):
        return remote(
            tail_out.at[j], tail_in.at[j], send_c.at[j], recv_c.at[j],
            {"az": lax.rem(az + 1, length)},
        )

    barrier = greet(
        [{"tile": lax.rem(me + k, tiles)} for k in range(1, tiles)]
        + [{"az": lax.rem(az + 1, length)}, {"az": lax.rem(az + length - 1, length)}]
    )
    get_scaling = pltpu.make_async_copy(scaling_ref, scaling, load.at[0])
    get_phase = pltpu.make_async_copy(azimuth_ref, phase, load.at[1])
    pl.semaphore_wait(barrier, tiles + 1)

    @pl.loop(0, spans)
    def _(j):
        for k in range(1, tiles):
            echo(j, k).start()
        keep_echo(j).start()

    @pl.loop(0, n_one)
    def _(g):
        load_piece(g).start()

    get_scaling.start()
    get_phase.start()

    @pl.loop(0, n_one)
    def _(g):
        load_piece(g).wait()

    permute_turn(o_ref, mid, turn)
    get_scaling.wait()

    @pl.loop(0, spans)
    def _(j):
        for k in range(1, tiles):
            echo(j, k).wait_recv()
        keep_echo(j).wait()
        hi, lo = front_ref[0], front_ref[1]
        z = []
        for e in range(4):
            rows = pl.ds(e, q, stride=4)
            s = jnp.concatenate([cols[j, 0, rows, :], cols[j, 1, rows, :]], axis=0)
            s_hi, s_lo = split(s)
            r = mm(hi, s_hi) + mm(hi, s_lo) + mm(lo, s_hi)
            r = (r[:m], r[m:])
            if e:
                r = times(r, (twist_ref[0, e], -twist_ref[1, e]))
            z.append(r)
        for f, x in enumerate(four(z, -1)):
            rows = pl.ds(f * m, m)
            x = times(x, sincos(scaling[rows, lanes(j)]))
            spec[0, rows, lanes(j)] = x[0]
            spec[1, rows, lanes(j)] = x[1]

    @pl.loop(0, blocks)
    def _(i):
        for k in range(1, tiles):
            out(i, k).start()

    first = pltpu.make_async_copy(spec.at[:, own, :], dop.at[:, :, mine], local_a)
    first.start()
    first.wait()

    @pl.loop(0, blocks)
    def _(i):
        if early:
            @pl.when(i == blocks - 1)
            def _():
                for k in range(1, tiles):
                    first_rows(k).start()

        for k in range(1, tiles):
            out(i, k).wait_recv()
        filter_rows(
            dop, i * block, block, fwd_ref, inv_ref, range_twist_ref, turn,
            hi_ref, lo_ref, mid,
        )

    for k in range(1, tiles):
        last_rows(k).start()
    keep(0).start()

    @pl.loop(1, spans)
    def _(j):
        for k in range(1, tiles):
            back(j, k).start()
        keep(j).start()

    get_phase.wait()

    @pl.loop(0, spans)
    def _(j):
        @pl.when(j == 0)
        def _():
            for k in range(1, tiles):
                if early:
                    first_rows(k).wait_recv()
                last_rows(k).wait_recv()

        @pl.when(j > 0)
        def _():
            for k in range(1, tiles):
                back(j, k).wait_recv()

        keep(j).wait()
        hi, lo = table_ref[0], table_ref[1]
        v = []
        for f in range(4):
            rows = pl.ds(f * m, m)
            v.append(times((ret[j, 0, rows, :], ret[j, 1, rows, :]), sincos(phase[rows, lanes(j)])))
        for e, x in enumerate(four(v, 1)):
            if e:
                x = times(x, (twist_ref[0, e], twist_ref[1, e]))
            s_hi, s_lo = split(jnp.concatenate(x, axis=0))
            r = mm(hi, s_hi) + mm(hi, s_lo) + mm(lo, s_hi)
            for c in (0, 1):
                head[c, pl.ds(e, q, stride=4), :] = r[c * m : c * m + q]
                tail_out[j, c, pl.ds(e, m - q, stride=4), :] = r[c * m + q : (c + 1) * m]

        @pl.when(az < length - 1)
        def _():
            onward(j).start()

        o_ref[:, :, lanes(j)] = head[...]

    @pl.when(az > 0)
    def _():
        @pl.loop(0, spans)
        def _(j):
            onward(j).wait_recv()
            o_ref[:, pl.ds(0, tail), lanes(j)] += tail_in[j]

    @pl.loop(0, blocks)
    def _(i):
        for k in range(1, tiles):
            out(i, k).wait_send()

    for k in range(1, tiles):
        if early:
            first_rows(k).wait_send()
        last_rows(k).wait_send()

    @pl.loop(1, spans)
    def _(j):
        for k in range(1, tiles):
            back(j, k).wait_send()

    @pl.loop(0, spans)
    def _(j):
        for k in range(1, tiles):
            echo(j, k).wait_send()

    @pl.when(az < length - 1)
    def _():
        @pl.loop(0, spans)
        def _(j):
            onward(j).wait_send()


def body(raw_echo, phase_scaling, phase_range, phase_azimuth):
    tiles = lax.axis_size("tile")
    length = lax.axis_size("az")
    pulses = raw_echo.shape[1] * tiles
    extent, width = phase_scaling.shape
    count, ranges = phase_range.shape
    m, q, tail = extent // 4, pulses // 4, extent - pulses
    n_one, spans = ranges // LANES, width // LANES
    block = min(64, count)
    rows, lane = np.arange(m), np.arange(LANES)
    vmem = pl.BlockSpec(memory_space=pltpu.VMEM)
    anyspace = pl.BlockSpec(memory_space=pl.ANY)
    dma = pltpu.SemaphoreType.DMA
    c, s = roots(np.arange(n_one), lane, ranges, -1)
    return pl.pallas_call(
        functools.partial(focus_kernel, tiles, length, block),
        out_shape=jax.ShapeDtypeStruct((2, pulses, width), F32),
        in_specs=[anyspace] * 4 + [vmem] * 6,
        out_specs=vmem,
        scratch_shapes=[
            pltpu.VMEM((2, extent, width), F32),
            pltpu.VMEM((extent, width), F32),
            pltpu.VMEM((n_one, count, LANES), F32),
            pltpu.VMEM((extent, width), F32),
            pltpu.VMEM((2, count, ranges), F32),
            pltpu.VMEM((spans, 2, extent, LANES), F32),
            pltpu.VMEM((spans, 2, max(tail, pulses), LANES), F32),
            pltpu.VMEM((spans, 2, tail, LANES), F32),
            pltpu.VMEM((2, pulses, LANES), F32),
            pltpu.VMEM((n_one, block, 2 * LANES), BF16),
            pltpu.VMEM((n_one, block, 2 * LANES), BF16),
            pltpu.VMEM((2, n_one * block, LANES), F32),
            dma((spans, tiles - 1)),
            dma((spans, tiles - 1)),
            dma((spans,)),
            dma((count // block, tiles - 1)),
            dma((count // block, tiles - 1)),
            dma,
            dma((spans + 1, tiles - 1)),
            dma((spans + 1, tiles - 1)),
            dma((spans,)),
            dma((spans,)),
            dma((spans,)),
            dma((2,)),
            dma((n_one,)),
        ],
        compiler_params=pltpu.CompilerParams(
            collective_id=0, has_side_effects=True, vmem_limit_bytes=63 << 20
        ),
    )(
        raw_echo,
        phase_scaling,
        phase_range,
        phase_azimuth,
        left_table(rows, np.arange(q), m, -1),
        twist_table(4, m, extent, 1),
        right_table(lane, lane, LANES, -1),
        right_table(lane, lane, LANES, 1, 1.0 / ranges),
        np.stack([c, s]).astype(np.float32),
        left_table(rows, rows, m, 1, 1.0 / extent),
    )


def solution(mesh):
    return jax.shard_map(
        body,
        mesh=mesh,
        in_specs=(
            P(None, ("strip", "az", "tile"), None),
            P(None, "tile"),
            P("tile", None),
            P(None, "tile"),
        ),
        out_specs=P(None, ("strip", "az"), "tile"),
        check_vma=False,
    )
```

```python
import functools
import math

import jax
import jax.numpy as jnp
import numpy as np
from jax import lax
from jax.experimental import pallas as pl
from jax.experimental.pallas import tpu as pltpu
from jax.sharding import PartitionSpec as P

F32 = jnp.float32
BF16 = jnp.bfloat16
LANES = 128


def halves(table):
    hi = np.asarray(table, np.float32).astype(jnp.bfloat16)
    lo = (np.asarray(table, np.float64) - hi.astype(np.float64)).astype(jnp.bfloat16)
    return np.stack([hi, lo])


def roots(rows, cols, modulus, direction):
    residue = np.outer(rows, cols) % modulus
    angle = residue * (direction * 2.0 * math.pi / modulus)
    return np.cos(angle), np.sin(angle)


def left_table(rows, cols, modulus, direction, scale=1.0):
    c, s = roots(rows, cols, modulus, direction)
    return halves(np.block([[c, -s], [s, c]]) * scale)


def right_table(rows, cols, modulus, direction, scale=1.0):
    c, s = roots(rows, cols, modulus, direction)
    return halves(np.block([[c, s], [-s, c]]) * scale)


def twist_table(count, length, modulus, direction):
    c, s = roots(np.arange(count), np.arange(length), modulus, direction)
    full = np.stack([c, s]).astype(np.float32)
    return np.ascontiguousarray(np.broadcast_to(full[..., None], full.shape + (LANES,)))


def split(x):
    hi = x.astype(BF16)
    return hi, (x - hi.astype(F32)).astype(BF16)


def mm(a, b):
    return jnp.dot(a, b, preferred_element_type=F32)


def times(a, t):
    return a[0] * t[0] - a[1] * t[1], a[0] * t[1] + a[1] * t[0]


def plus(a, b):
    return a[0] + b[0], a[1] + b[1]


def minus(a, b):
    return a[0] - b[0], a[1] - b[1]


def quarter(a, direction):
    return (-a[1], a[0]) if direction > 0 else (a[1], -a[0])


def four(v, direction):
    a, b = plus(v[0], v[2]), minus(v[0], v[2])
    c, d = plus(v[1], v[3]), quarter(minus(v[1], v[3]), direction)
    return [plus(a, c), plus(b, d), minus(a, c), minus(b, d)]


def fft(v, direction):
    n = len(v)
    if n == 1:
        return v
    if n == 2:
        return [plus(v[0], v[1]), minus(v[0], v[1])]
    if n == 4:
        return four(v, direction)
    parts = [fft(v[e::4], direction) for e in range(4)] if n % 4 == 0 else None
    out = [None] * n
    m = n // 4
    for f in range(m):
        items = []
        for e in range(4):
            x = parts[e][f]
            k = e * f % n
            if k == 0:
                pass
            elif 8 * k == n:
                h = np.float32(math.sqrt(0.5))
                q = quarter(x, direction)
                x = ((x[0] + q[0]) * h, (x[1] + q[1]) * h)
            elif 4 * k == n:
                x = quarter(x, direction)
            elif 8 * k == 3 * n:
                h = np.float32(math.sqrt(0.5))
                q = quarter(x, direction)
                x = ((q[0] - x[0]) * h, (q[1] - x[1]) * h)
            else:
                ang = direction * 2.0 * math.pi * k / n
                x = times(x, (np.float32(math.cos(ang)), np.float32(math.sin(ang))))
            items.append(x)
        got = four(items, direction)
        for j in range(4):
            out[f + j * m] = got[j]
    return out


def sincos(x):
    y = x * 0.5
    z = y * y
    s, c = -1.0 / 39916800, 1.0 / 479001600
    for a, b in ((362880, -3628800), (-5040, 40320), (120, -720), (-6, 24), (1, -2)):
        s = s * z + np.float32(1.0 / a)
        c = c * z + np.float32(1.0 / b)
    s = s * y
    c = c * z + 1.0
    return 1.0 - 2.0 * s * s, 2.0 * s * c


def greet(partners):
    barrier = pltpu.get_barrier_semaphore()
    for device in partners:
        pl.semaphore_signal(barrier, inc=1, device_id=device, device_id_type=pl.DeviceIdType.MESH)
    return barrier


def lanes(j):
    return pl.ds(pl.multiple_of(j * LANES, LANES), LANES)


def filter_rows(x_ref, base, block, fwd_ref, inv_ref, twist_ref, phase_ref, hi_ref, lo_ref, mid_ref):
    n_one = phase_ref.shape[0]
    step = 16
    f_hi, f_lo = fwd_ref[0], fwd_ref[1]
    b_hi, b_lo = inv_ref[0], inv_ref[1]

    @pl.loop(0, block // step)
    def _(i):
        rows = pl.ds(pl.multiple_of(i * step, step), step)
        at = pl.ds(pl.multiple_of(base + i * step, step), step)
        v = [
            tuple(x_ref[c, at, pl.ds(a * LANES, LANES)] for c in (0, 1))
            for a in range(n_one)
        ]
        for k, x in enumerate(fft(v, -1)):
            if k:
                x = times(x, (twist_ref[0, k : k + 1, :], twist_ref[1, k : k + 1, :]))
            for c in (0, 1):
                h, l = split(x[c])
                hi_ref[k, rows, pl.ds(c * LANES, LANES)] = h
                lo_ref[k, rows, pl.ds(c * LANES, LANES)] = l

    group = 4

    @pl.loop(0, n_one // group)
    def _(i):
        ks = pl.ds(i * group, group)
        flat = (group * block, 2 * LANES)
        h, l = hi_ref[ks].reshape(flat), lo_ref[ks].reshape(flat)
        r = mm(h, f_hi) + mm(l, f_hi) + mm(h, f_lo)
        turn = phase_ref[ks, pl.ds(pl.multiple_of(base, block), block), :]
        r = times((r[:, :LANES], r[:, LANES:]), sincos(turn.reshape(group * block, LANES)))
        h, l = split(jnp.concatenate(r, axis=1))
        r = mm(h, b_hi) + mm(l, b_hi) + mm(h, b_lo)
        at = pl.ds(pl.multiple_of(i * group * block, block), group * block)
        mid_ref[0, at, :] = r[:, :LANES]
        mid_ref[1, at, :] = r[:, LANES:]

    @pl.loop(0, block // 8)
    def _(i):
        at = pl.ds(pl.multiple_of(base + i * 8, 8), 8)
        v = []
        for k in range(n_one):
            x = tuple(mid_ref[c, pl.ds(pl.multiple_of(k * block + i * 8, 8), 8), :] for c in (0, 1))
            if k:
                x = times(x, (twist_ref[0, k : k + 1, :], -twist_ref[1, k : k + 1, :]))
            v.append(x)
        for a, x in enumerate(fft(v, 1)):
            for c in (0, 1):
                x_ref[c, at, pl.ds(a * LANES, LANES)] = x[c]


def permute_turn(o_ref, mid, turn):
    n_one, count, _ = turn.shape
    half = mid.shape[1]
    some = min(count, LANES)
    part = half // n_one

    @pl.loop(0, count // some)
    def _(i):
        @pl.loop(0, n_one)
        def _(g):
            c, row, j = piece(g, count, o_ref)
            at = pl.ds(pl.multiple_of(row + i * some, some), some)
            x = o_ref[c, at, lanes(j)]
            if some < LANES:
                x = jnp.concatenate([x] * (LANES // some), axis=0)
            per = half // LANES
            mid[g // per, pl.ds(pl.multiple_of(g % per * LANES, LANES), LANES), :] = x.T

        @pl.loop(0, n_one)
        def _(k):
            rows = pl.ds(k, part, stride=n_one)
            x = jnp.concatenate([mid[h, rows, :] for h in range(LANES // part)], axis=0)
            at = pl.ds(pl.multiple_of(i * some, some), some)
            turn[k, at, :] = x.T[:some]


def piece(g, count, o_ref):
    across = o_ref.shape[2] // LANES
    down = o_ref.shape[1] // count
    return g // (across * down), g // across % down * count, g % across


def focus_kernel(
    tiles, length, block,
    raw_ref, scaling_ref, range_ref, azimuth_ref,
    front_ref, twist_ref, fwd_ref, inv_ref, range_twist_ref, table_ref,
    o_ref, tail_in,
    spec, scaling, turn, phase, dop, ret, tail_out, head, hi_ref, lo_ref, mid,
    send_e, recv_e, local_e, send_a, recv_a, local_a, send_b, recv_b, local_b,
    send_c, recv_c, load, load_range,
):
    me = lax.axis_index("tile")
    az = lax.axis_index("az")
    count = dop.shape[1]
    width = o_ref.shape[2]
    pulses = o_ref.shape[1]
    tail = tail_in.shape[1]
    rows_own = raw_ref.shape[1]
    n_one = turn.shape[0]
    blocks = count // block
    early = (blocks - 1) * block
    spans = width // LANES
    cols = tail_out
    m = spec.shape[1] // 4
    q = pulses // 4
    mine = pl.ds(pl.multiple_of(me * width, LANES), width)
    own = pl.ds(pl.multiple_of(me * count, count), count)
    own_pulses = pl.ds(pl.multiple_of(me * rows_own, rows_own), rows_own)

    def remote(src, dst, send, recv, device):
        return pltpu.make_async_remote_copy(
            src_ref=src, dst_ref=dst, send_sem=send, recv_sem=recv,
            device_id=device, device_id_type=pl.DeviceIdType.MESH,
        )

    def echo(j, k):
        to = lax.rem(me + k, tiles)
        return remote(
            raw_ref.at[:, :, lanes(to * spans + j)], cols.at[j, :, own_pulses, :],
            send_e.at[j, k - 1], recv_e.at[j, k - 1], {"tile": to},
        )

    def keep_echo(j):
        return pltpu.make_async_copy(
            raw_ref.at[:, :, lanes(me * spans + j)], cols.at[j, :, own_pulses, :], local_e.at[j]
        )

    def load_piece(g):
        c, row, j = piece(g, count, o_ref)
        return pltpu.make_async_copy(
            range_ref.at[:, lanes(g)],
            o_ref.at[c, pl.ds(pl.multiple_of(row, count), count), lanes(j)],
            load_range.at[g],
        )

    def out_part(i, k, lo, n, slot):
        to = lax.rem(me + k, tiles)
        at = pl.ds(pl.multiple_of(me * width + lo, LANES), n)
        return remote(
            spec.at[:, pl.ds(pl.multiple_of(to * count + i * block, block), block), pl.ds(lo, n)],
            dop.at[:, pl.ds(pl.multiple_of(i * block, block), block), at],
            send_a.at[slot, k - 1], recv_a.at[slot, k - 1], {"tile": to},
        )

    def out(i, k):
        return out_part(i, k, 0, width, i)

    def first_out(k):
        return out_part(0, k, 0, width - LANES, blocks)

    def last_out(k):
        return out_part(0, k, width - LANES, LANES, 0)

    def back_rows(j, k, lo, n, slot):
        to = lax.rem(me + k, tiles)
        return remote(
            dop.at[:, pl.ds(lo, n), lanes(to * spans + j)],
            ret.at[j, :, pl.ds(pl.multiple_of(me * count + lo, 8), n), :],
            send_b.at[slot, k - 1], recv_b.at[slot, k - 1], {"tile": to},
        )

    def first_rows(k):
        return back_rows(0, k, 0, early, spans)

    def last_rows(k):
        return back_rows(0, k, early, count - early, 0)

    def back(j, k):
        return back_rows(j, k, 0, count, j)

    def keep(j):
        return pltpu.make_async_copy(
            dop.at[:, :, lanes(me * spans + j)], ret.at[j, :, own, :], local_b.at[j]
        )

    def onward(j):
        return remote(
            tail_out.at[j, :, pl.ds(0, tail), :], tail_in.at[:, :, lanes(j)], send_c.at[j], recv_c.at[j],
            {"az": lax.rem(az + 1, length)},
        )

    barrier = greet(
        [{"tile": lax.rem(me + k, tiles)} for k in range(1, tiles)]
        + [{"az": lax.rem(az + 1, length)}, {"az": lax.rem(az + length - 1, length)}]
    )
    get_scaling = pltpu.make_async_copy(scaling_ref, scaling, load.at[0])
    get_phase = pltpu.make_async_copy(azimuth_ref, phase, load.at[1])
    pl.semaphore_wait(barrier, tiles + 1)

    @pl.loop(0, spans)
    def _(j):
        for k in range(1, tiles):
            echo(j, k).start()
        keep_echo(j).start()

    @pl.loop(0, n_one)
    def _(g):
        load_piece(g).start()

    get_scaling.start()
    get_phase.start()

    @pl.loop(0, n_one)
    def _(g):
        load_piece(g).wait()

    permute_turn(o_ref, mid, turn)
    get_scaling.wait()

    @pl.loop(0, spans)
    def _(j):
        @pl.when(j == spans - 1)
        def _():
            for k in range(1, tiles):
                first_out(k).start()

        for k in range(1, tiles):
            echo(j, k).wait_recv()
        keep_echo(j).wait()
        hi, lo = front_ref[0], front_ref[1]
        z = []
        for e in range(4):
            rows = pl.ds(e, q, stride=4)
            s = jnp.concatenate([cols[j, 0, rows, :], cols[j, 1, rows, :]], axis=0)
            s_hi, s_lo = split(s)
            r = mm(hi, s_hi) + mm(hi, s_lo) + mm(lo, s_hi)
            r = (r[:m], r[m:])
            if e:
                r = times(r, (twist_ref[0, e], -twist_ref[1, e]))
            z.append(r)
        for f, x in enumerate(four(z, -1)):
            rows = pl.ds(f * m, m)
            x = times(x, sincos(scaling[rows, lanes(j)]))
            spec[0, rows, lanes(j)] = x[0]
            spec[1, rows, lanes(j)] = x[1]

    for k in range(1, tiles):
        last_out(k).start()

    @pl.loop(1, blocks)
    def _(i):
        for k in range(1, tiles):
            out(i, k).start()

    first = pltpu.make_async_copy(spec.at[:, own, :], dop.at[:, :, mine], local_a)
    first.start()
    first.wait()

    @pl.loop(0, blocks)
    def _(i):
        if early:
            @pl.when(i == blocks - 1)
            def _():
                for k in range(1, tiles):
                    first_rows(k).start()

        @pl.when(i == 0)
        def _():
            for k in range(1, tiles):
                first_out(k).wait_recv()
                last_out(k).wait_recv()

        @pl.when(i > 0)
        def _():
            for k in range(1, tiles):
                out(i, k).wait_recv()

        filter_rows(
            dop, i * block, block, fwd_ref, inv_ref, range_twist_ref, turn,
            hi_ref, lo_ref, mid,
        )

    for k in range(1, tiles):
        last_rows(k).start()
    keep(0).start()

    @pl.loop(1, spans)
    def _(j):
        for k in range(1, tiles):
            back(j, k).start()
        keep(j).start()

    get_phase.wait()

    @pl.loop(0, spans)
    def _(j):
        @pl.when(j == 0)
        def _():
            for k in range(1, tiles):
                if early:
                    first_rows(k).wait_recv()
                last_rows(k).wait_recv()

        @pl.when(j > 0)
        def _():
            for k in range(1, tiles):
                back(j, k).wait_recv()

        keep(j).wait()
        hi, lo = table_ref[0], table_ref[1]
        v = []
        for f in range(4):
            rows = pl.ds(f * m, m)
            v.append(times((ret[j, 0, rows, :], ret[j, 1, rows, :]), sincos(phase[rows, lanes(j)])))
        for e, x in enumerate(four(v, 1)):
            if e:
                x = times(x, (twist_ref[0, e], twist_ref[1, e]))
            s_hi, s_lo = split(jnp.concatenate(x, axis=0))
            r = mm(hi, s_hi) + mm(hi, s_lo) + mm(lo, s_hi)
            for c in (0, 1):
                head[c, pl.ds(e, q, stride=4), :] = r[c * m : c * m + q]
                tail_out[j, c, pl.ds(e, m - q, stride=4), :] = r[c * m + q : (c + 1) * m]

        @pl.when(az < length - 1)
        def _():
            onward(j).start()

        o_ref[:, :, lanes(j)] = head[...]

    @pl.when(az > 0)
    def _():
        @pl.loop(0, spans)
        def _(j):
            onward(j).wait_recv()

    for k in range(1, tiles):
        first_out(k).wait_send()
        last_out(k).wait_send()

    @pl.loop(1, blocks)
    def _(i):
        for k in range(1, tiles):
            out(i, k).wait_send()

    for k in range(1, tiles):
        if early:
            first_rows(k).wait_send()
        last_rows(k).wait_send()

    @pl.loop(1, spans)
    def _(j):
        for k in range(1, tiles):
            back(j, k).wait_send()

    @pl.loop(0, spans)
    def _(j):
        for k in range(1, tiles):
            echo(j, k).wait_send()

    @pl.when(az < length - 1)
    def _():
        @pl.loop(0, spans)
        def _(j):
            onward(j).wait_send()


def body(raw_echo, phase_scaling, phase_range, phase_azimuth):
    tiles = lax.axis_size("tile")
    length = lax.axis_size("az")
    pulses = raw_echo.shape[1] * tiles
    extent, width = phase_scaling.shape
    count, ranges = phase_range.shape
    m, q, tail = extent // 4, pulses // 4, extent - pulses
    n_one, spans = ranges // LANES, width // LANES
    block = min(64, count)
    rows, lane = np.arange(m), np.arange(LANES)
    vmem = pl.BlockSpec(memory_space=pltpu.VMEM)
    anyspace = pl.BlockSpec(memory_space=pl.ANY)
    dma = pltpu.SemaphoreType.DMA
    c, s = roots(np.arange(n_one), lane, ranges, -1)
    head, incoming = pl.pallas_call(
        functools.partial(focus_kernel, tiles, length, block),
        out_shape=[
            jax.ShapeDtypeStruct((2, pulses, width), F32),
            jax.ShapeDtypeStruct((2, tail, width), F32),
        ],
        in_specs=[anyspace] * 4 + [vmem] * 6,
        out_specs=[vmem, anyspace],
        scratch_shapes=[
            pltpu.VMEM((2, extent, width), F32),
            pltpu.VMEM((extent, width), F32),
            pltpu.VMEM((n_one, count, LANES), F32),
            pltpu.VMEM((extent, width), F32),
            pltpu.VMEM((2, count, ranges), F32),
            pltpu.VMEM((spans, 2, extent, LANES), F32),
            pltpu.VMEM((spans, 2, max(tail, pulses), LANES), F32),
            pltpu.VMEM((2, pulses, LANES), F32),
            pltpu.VMEM((n_one, block, 2 * LANES), BF16),
            pltpu.VMEM((n_one, block, 2 * LANES), BF16),
            pltpu.VMEM((2, n_one * block, LANES), F32),
            dma((spans, tiles - 1)),
            dma((spans, tiles - 1)),
            dma((spans,)),
            dma((count // block + 1, tiles - 1)),
            dma((count // block + 1, tiles - 1)),
            dma,
            dma((spans + 1, tiles - 1)),
            dma((spans + 1, tiles - 1)),
            dma((spans,)),
            dma((spans,)),
            dma((spans,)),
            dma((2,)),
            dma((n_one,)),
        ],
        compiler_params=pltpu.CompilerParams(
            collective_id=0, has_side_effects=True, vmem_limit_bytes=63 << 20
        ),
    )(
        raw_echo,
        phase_scaling,
        phase_range,
        phase_azimuth,
        left_table(rows, np.arange(q), m, -1),
        twist_table(4, m, extent, 1),
        right_table(lane, lane, LANES, -1),
        right_table(lane, lane, LANES, 1, 1.0 / ranges),
        np.stack([c, s]).astype(np.float32),
        left_table(rows, rows, m, 1, 1.0 / extent),
    )
    joined = head[:, :tail] + incoming
    if tail < pulses:
        joined = jnp.concatenate([joined, head[:, tail:]], axis=1)
    return jnp.where(lax.axis_index("az") > 0, joined, head)


def solution(mesh):
    return jax.shard_map(
        body,
        mesh=mesh,
        in_specs=(
            P(None, ("strip", "az", "tile"), None),
            P(None, "tile"),
            P("tile", None),
            P(None, "tile"),
        ),
        out_specs=P(None, ("strip", "az"), "tile"),
        check_vma=False,
    )
```

```python
import functools
import math

import jax
import jax.numpy as jnp
import numpy as np
from jax import lax
from jax.experimental import pallas as pl
from jax.experimental.pallas import tpu as pltpu
from jax.sharding import PartitionSpec as P

F32 = jnp.float32
BF16 = jnp.bfloat16
LANES = 128


def halves(table):
    hi = np.asarray(table, np.float32).astype(jnp.bfloat16)
    lo = (np.asarray(table, np.float64) - hi.astype(np.float64)).astype(jnp.bfloat16)
    return np.stack([hi, lo])


def roots(rows, cols, modulus, direction):
    residue = np.outer(rows, cols) % modulus
    angle = residue * (direction * 2.0 * math.pi / modulus)
    return np.cos(angle), np.sin(angle)


def left_table(rows, cols, modulus, direction, scale=1.0):
    c, s = roots(rows, cols, modulus, direction)
    return halves(np.block([[c, -s], [s, c]]) * scale)


def right_table(rows, cols, modulus, direction, scale=1.0):
    c, s = roots(rows, cols, modulus, direction)
    return halves(np.block([[c, s], [-s, c]]) * scale)


def twist_table(count, length, modulus, direction):
    c, s = roots(np.arange(count), np.arange(length), modulus, direction)
    full = np.stack([c, s]).astype(np.float32)
    return np.ascontiguousarray(np.broadcast_to(full[..., None], full.shape + (LANES,)))


def split(x):
    hi = x.astype(BF16)
    return hi, (x - hi.astype(F32)).astype(BF16)


def mm(a, b):
    return jnp.dot(a, b, preferred_element_type=F32)


def times(a, t):
    return a[0] * t[0] - a[1] * t[1], a[0] * t[1] + a[1] * t[0]


def plus(a, b):
    return a[0] + b[0], a[1] + b[1]


def minus(a, b):
    return a[0] - b[0], a[1] - b[1]


def quarter(a, direction):
    return (-a[1], a[0]) if direction > 0 else (a[1], -a[0])


def four(v, direction):
    a, b = plus(v[0], v[2]), minus(v[0], v[2])
    c, d = plus(v[1], v[3]), quarter(minus(v[1], v[3]), direction)
    return [plus(a, c), plus(b, d), minus(a, c), minus(b, d)]


def fft(v, direction):
    n = len(v)
    if n == 1:
        return v
    if n == 2:
        return [plus(v[0], v[1]), minus(v[0], v[1])]
    if n == 4:
        return four(v, direction)
    parts = [fft(v[e::4], direction) for e in range(4)] if n % 4 == 0 else None
    out = [None] * n
    m = n // 4
    for f in range(m):
        items = []
        for e in range(4):
            x = parts[e][f]
            k = e * f % n
            if k == 0:
                pass
            elif 8 * k == n:
                h = np.float32(math.sqrt(0.5))
                q = quarter(x, direction)
                x = ((x[0] + q[0]) * h, (x[1] + q[1]) * h)
            elif 4 * k == n:
                x = quarter(x, direction)
            elif 8 * k == 3 * n:
                h = np.float32(math.sqrt(0.5))
                q = quarter(x, direction)
                x = ((q[0] - x[0]) * h, (q[1] - x[1]) * h)
            else:
                ang = direction * 2.0 * math.pi * k / n
                x = times(x, (np.float32(math.cos(ang)), np.float32(math.sin(ang))))
            items.append(x)
        got = four(items, direction)
        for j in range(4):
            out[f + j * m] = got[j]
    return out


def sincos(x):
    y = x * 0.5
    z = y * y
    s, c = -1.0 / 39916800, 1.0 / 479001600
    for a, b in ((362880, -3628800), (-5040, 40320), (120, -720), (-6, 24), (1, -2)):
        s = s * z + np.float32(1.0 / a)
        c = c * z + np.float32(1.0 / b)
    s = s * y
    c = c * z + 1.0
    return 1.0 - 2.0 * s * s, 2.0 * s * c


def greet(partners):
    barrier = pltpu.get_barrier_semaphore()
    for device in partners:
        pl.semaphore_signal(barrier, inc=1, device_id=device, device_id_type=pl.DeviceIdType.MESH)
    return barrier


def lanes(j):
    return pl.ds(pl.multiple_of(j * LANES, LANES), LANES)


def filter_rows(x_ref, base, block, fwd_ref, inv_ref, twist_ref, phase_ref, hi_ref, lo_ref, mid_ref):
    n_one = phase_ref.shape[0]
    step = 16
    f_hi, f_lo = fwd_ref[0], fwd_ref[1]
    b_hi, b_lo = inv_ref[0], inv_ref[1]

    @pl.loop(0, block // step)
    def _(i):
        rows = pl.ds(pl.multiple_of(i * step, step), step)
        at = pl.ds(pl.multiple_of(base + i * step, step), step)
        v = [
            tuple(x_ref[c, at, pl.ds(a * LANES, LANES)] for c in (0, 1))
            for a in range(n_one)
        ]
        for k, x in enumerate(fft(v, -1)):
            if k:
                x = times(x, (twist_ref[0, k : k + 1, :], twist_ref[1, k : k + 1, :]))
            for c in (0, 1):
                h, l = split(x[c])
                hi_ref[k, rows, pl.ds(c * LANES, LANES)] = h
                lo_ref[k, rows, pl.ds(c * LANES, LANES)] = l

    group = 4

    @pl.loop(0, n_one // group)
    def _(i):
        ks = pl.ds(i * group, group)
        flat = (group * block, 2 * LANES)
        h, l = hi_ref[ks].reshape(flat), lo_ref[ks].reshape(flat)
        r = mm(h, f_hi) + mm(l, f_hi) + mm(h, f_lo)
        turn = phase_ref[ks, pl.ds(pl.multiple_of(base, block), block), :]
        r = times((r[:, :LANES], r[:, LANES:]), sincos(turn.reshape(group * block, LANES)))
        h, l = split(jnp.concatenate(r, axis=1))
        r = mm(h, b_hi) + mm(l, b_hi) + mm(h, b_lo)
        at = pl.ds(pl.multiple_of(i * group * block, block), group * block)
        mid_ref[0, at, :] = r[:, :LANES]
        mid_ref[1, at, :] = r[:, LANES:]

    @pl.loop(0, block // 8)
    def _(i):
        at = pl.ds(pl.multiple_of(base + i * 8, 8), 8)
        v = []
        for k in range(n_one):
            x = tuple(mid_ref[c, pl.ds(pl.multiple_of(k * block + i * 8, 8), 8), :] for c in (0, 1))
            if k:
                x = times(x, (twist_ref[0, k : k + 1, :], -twist_ref[1, k : k + 1, :]))
            v.append(x)
        for a, x in enumerate(fft(v, 1)):
            for c in (0, 1):
                x_ref[c, at, pl.ds(a * LANES, LANES)] = x[c]


def permute_turn(o_ref, mid, turn):
    n_one, count, _ = turn.shape
    half = mid.shape[1]
    some = min(count, LANES)
    part = half // n_one

    @pl.loop(0, count // some)
    def _(i):
        @pl.loop(0, n_one)
        def _(g):
            c, row, j = piece(g, count, o_ref)
            at = pl.ds(pl.multiple_of(row + i * some, some), some)
            x = o_ref[c, at, lanes(j)]
            if some < LANES:
                x = jnp.concatenate([x] * (LANES // some), axis=0)
            per = half // LANES
            mid[g // per, pl.ds(pl.multiple_of(g % per * LANES, LANES), LANES), :] = x.T

        @pl.loop(0, n_one)
        def _(k):
            rows = pl.ds(k, part, stride=n_one)
            x = jnp.concatenate([mid[h, rows, :] for h in range(LANES // part)], axis=0)
            at = pl.ds(pl.multiple_of(i * some, some), some)
            turn[k, at, :] = x.T[:some]


def piece(g, count, o_ref):
    across = o_ref.shape[2] // LANES
    down = o_ref.shape[1] // count
    return g // (across * down), g // across % down * count, g % across


def focus_kernel(
    tiles, length, block,
    raw_ref, scaling_ref, range_ref, azimuth_ref,
    front_ref, twist_ref, fwd_ref, inv_ref, range_twist_ref, table_ref,
    o_ref,
    spec, scaling, turn, phase, dop, ret, tail_out, tail_in, head, hi_ref, lo_ref, mid,
    send_e, recv_e, local_e, send_a, recv_a, local_a, send_b, recv_b, local_b,
    send_c, recv_c, load, load_range,
):
    me = lax.axis_index("tile")
    az = lax.axis_index("az")
    count = dop.shape[1]
    width = o_ref.shape[2]
    pulses = o_ref.shape[1]
    tail = tail_in.shape[2]
    rows_own = raw_ref.shape[1]
    n_one = turn.shape[0]
    blocks = count // block
    early = (blocks - 1) * block
    spans = width // LANES
    cols = tail_out
    m = spec.shape[1] // 4
    q = pulses // 4
    mine = pl.ds(pl.multiple_of(me * width, LANES), width)
    own = pl.ds(pl.multiple_of(me * count, count), count)
    own_pulses = pl.ds(pl.multiple_of(me * rows_own, rows_own), rows_own)

    def remote(src, dst, send, recv, device):
        return pltpu.make_async_remote_copy(
            src_ref=src, dst_ref=dst, send_sem=send, recv_sem=recv,
            device_id=device, device_id_type=pl.DeviceIdType.MESH,
        )

    def echo(j, k):
        to = lax.rem(me + k, tiles)
        return remote(
            raw_ref.at[:, :, lanes(to * spans + j)], cols.at[j, :, own_pulses, :],
            send_e.at[j, k - 1], recv_e.at[j, k - 1], {"tile": to},
        )

    def keep_echo(j):
        return pltpu.make_async_copy(
            raw_ref.at[:, :, lanes(me * spans + j)], cols.at[j, :, own_pulses, :], local_e.at[j]
        )

    def load_piece(g):
        c, row, j = piece(g, count, o_ref)
        return pltpu.make_async_copy(
            range_ref.at[:, lanes(g)],
            o_ref.at[c, pl.ds(pl.multiple_of(row, count), count), lanes(j)],
            load_range.at[g],
        )

    def out_part(i, k, lo, n, slot):
        to = lax.rem(me + k, tiles)
        at = pl.ds(pl.multiple_of(me * width + lo, LANES), n)
        return remote(
            spec.at[:, pl.ds(pl.multiple_of(to * count + i * block, block), block), pl.ds(lo, n)],
            dop.at[:, pl.ds(pl.multiple_of(i * block, block), block), at],
            send_a.at[slot, k - 1], recv_a.at[slot, k - 1], {"tile": to},
        )

    def out(i, k):
        return out_part(i, k, 0, width, i)

    def first_out(k):
        return out_part(0, k, 0, width - LANES, blocks)

    def last_out(k):
        return out_part(0, k, width - LANES, LANES, 0)

    def back_rows(j, k, lo, n, slot):
        to = lax.rem(me + k, tiles)
        return remote(
            dop.at[:, pl.ds(lo, n), lanes(to * spans + j)],
            ret.at[j, :, pl.ds(pl.multiple_of(me * count + lo, 8), n), :],
            send_b.at[slot, k - 1], recv_b.at[slot, k - 1], {"tile": to},
        )

    def first_rows(k):
        return back_rows(0, k, 0, early, spans)

    def last_rows(k):
        return back_rows(0, k, early, count - early, 0)

    def back(j, k):
        return back_rows(j, k, 0, count, j)

    def keep(j):
        return pltpu.make_async_copy(
            dop.at[:, :, lanes(me * spans + j)], ret.at[j, :, own, :], local_b.at[j]
        )

    def onward(j):
        return remote(
            tail_out.at[j, :, pl.ds(0, tail), :], tail_in.at[j], send_c.at[j], recv_c.at[j],
            {"az": lax.rem(az + 1, length)},
        )

    barrier = greet(
        [{"tile": lax.rem(me + k, tiles)} for k in range(1, tiles)]
        + [{"az": lax.rem(az + 1, length)}, {"az": lax.rem(az + length - 1, length)}]
    )
    get_scaling = pltpu.make_async_copy(scaling_ref, scaling, load.at[0])
    get_phase = pltpu.make_async_copy(azimuth_ref, phase, load.at[1])
    pl.semaphore_wait(barrier, tiles + 1)

    @pl.loop(0, spans)
    def _(j):
        for k in range(1, tiles):
            echo(j, k).start()
        keep_echo(j).start()

    @pl.loop(0, n_one)
    def _(g):
        load_piece(g).start()

    get_scaling.start()
    get_phase.start()

    get_scaling.wait()

    @pl.loop(0, spans)
    def _(j):
        @pl.when(j == spans - 1)
        def _():
            for k in range(1, tiles):
                first_out(k).start()

        for k in range(1, tiles):
            echo(j, k).wait_recv()
        keep_echo(j).wait()
        hi, lo = front_ref[0], front_ref[1]
        z = []
        for e in range(4):
            rows = pl.ds(e, q, stride=4)
            s = jnp.concatenate([cols[j, 0, rows, :], cols[j, 1, rows, :]], axis=0)
            s_hi, s_lo = split(s)
            r = mm(hi, s_hi) + mm(hi, s_lo) + mm(lo, s_hi)
            r = (r[:m], r[m:])
            if e:
                r = times(r, (twist_ref[0, e], -twist_ref[1, e]))
            z.append(r)
        for f, x in enumerate(four(z, -1)):
            rows = pl.ds(f * m, m)
            x = times(x, sincos(scaling[rows, lanes(j)]))
            spec[0, rows, lanes(j)] = x[0]
            spec[1, rows, lanes(j)] = x[1]

    for k in range(1, tiles):
        last_out(k).start()

    @pl.loop(1, blocks)
    def _(i):
        for k in range(1, tiles):
            out(i, k).start()

    first = pltpu.make_async_copy(spec.at[:, own, :], dop.at[:, :, mine], local_a)
    first.start()

    @pl.loop(0, n_one)
    def _(g):
        load_piece(g).wait()

    permute_turn(o_ref, mid, turn)
    first.wait()

    @pl.loop(0, blocks)
    def _(i):
        if early:
            @pl.when(i == blocks - 1)
            def _():
                for k in range(1, tiles):
                    first_rows(k).start()

        @pl.when(i == 0)
        def _():
            for k in range(1, tiles):
                first_out(k).wait_recv()
                last_out(k).wait_recv()

        @pl.when(i > 0)
        def _():
            for k in range(1, tiles):
                out(i, k).wait_recv()

        filter_rows(
            dop, i * block, block, fwd_ref, inv_ref, range_twist_ref, turn,
            hi_ref, lo_ref, mid,
        )

    for k in range(1, tiles):
        last_rows(k).start()
    keep(0).start()

    @pl.loop(1, spans)
    def _(j):
        for k in range(1, tiles):
            back(j, k).start()
        keep(j).start()

    get_phase.wait()

    @pl.loop(0, spans)
    def _(j):
        @pl.when(j == 0)
        def _():
            for k in range(1, tiles):
                if early:
                    first_rows(k).wait_recv()
                last_rows(k).wait_recv()

        @pl.when(j > 0)
        def _():
            for k in range(1, tiles):
                back(j, k).wait_recv()

        keep(j).wait()
        hi, lo = table_ref[0], table_ref[1]
        v = []
        for f in range(4):
            rows = pl.ds(f * m, m)
            v.append(times((ret[j, 0, rows, :], ret[j, 1, rows, :]), sincos(phase[rows, lanes(j)])))
        for e, x in enumerate(four(v, 1)):
            if e:
                x = times(x, (twist_ref[0, e], twist_ref[1, e]))
            s_hi, s_lo = split(jnp.concatenate(x, axis=0))
            r = mm(hi, s_hi) + mm(hi, s_lo) + mm(lo, s_hi)
            for c in (0, 1):
                head[c, pl.ds(e, q, stride=4), :] = r[c * m : c * m + q]
                tail_out[j, c, pl.ds(e, m - q, stride=4), :] = r[c * m + q : (c + 1) * m]

        @pl.when(az < length - 1)
        def _():
            onward(j).start()

        o_ref[:, :, lanes(j)] = head[...]

    @pl.when(az > 0)
    def _():
        @pl.loop(0, spans)
        def _(j):
            onward(j).wait_recv()
            o_ref[:, pl.ds(0, tail), lanes(j)] += tail_in[j]

    for k in range(1, tiles):
        first_out(k).wait_send()
        last_out(k).wait_send()

    @pl.loop(1, blocks)
    def _(i):
        for k in range(1, tiles):
            out(i, k).wait_send()

    for k in range(1, tiles):
        if early:
            first_rows(k).wait_send()
        last_rows(k).wait_send()

    @pl.loop(1, spans)
    def _(j):
        for k in range(1, tiles):
            back(j, k).wait_send()

    @pl.loop(0, spans)
    def _(j):
        for k in range(1, tiles):
            echo(j, k).wait_send()

    @pl.when(az < length - 1)
    def _():
        @pl.loop(0, spans)
        def _(j):
            onward(j).wait_send()


def body(raw_echo, phase_scaling, phase_range, phase_azimuth):
    tiles = lax.axis_size("tile")
    length = lax.axis_size("az")
    pulses = raw_echo.shape[1] * tiles
    extent, width = phase_scaling.shape
    count, ranges = phase_range.shape
    m, q, tail = extent // 4, pulses // 4, extent - pulses
    n_one, spans = ranges // LANES, width // LANES
    block = min(64, count)
    rows, lane = np.arange(m), np.arange(LANES)
    vmem = pl.BlockSpec(memory_space=pltpu.VMEM)
    anyspace = pl.BlockSpec(memory_space=pl.ANY)
    dma = pltpu.SemaphoreType.DMA
    c, s = roots(np.arange(n_one), lane, ranges, -1)
    return pl.pallas_call(
        functools.partial(focus_kernel, tiles, length, block),
        out_shape=jax.ShapeDtypeStruct((2, pulses, width), F32),
        in_specs=[anyspace] * 4 + [vmem] * 6,
        out_specs=vmem,
        scratch_shapes=[
            pltpu.VMEM((2, extent, width), F32),
            pltpu.VMEM((extent, width), F32),
            pltpu.VMEM((n_one, count, LANES), F32),
            pltpu.VMEM((extent, width), F32),
            pltpu.VMEM((2, count, ranges), F32),
            pltpu.VMEM((spans, 2, extent, LANES), F32),
            pltpu.VMEM((spans, 2, max(tail, pulses), LANES), F32),
            pltpu.VMEM((spans, 2, tail, LANES), F32),
            pltpu.VMEM((2, pulses, LANES), F32),
            pltpu.VMEM((n_one, block, 2 * LANES), BF16),
            pltpu.VMEM((n_one, block, 2 * LANES), BF16),
            pltpu.VMEM((2, n_one * block, LANES), F32),
            dma((spans, tiles - 1)),
            dma((spans, tiles - 1)),
            dma((spans,)),
            dma((count // block + 1, tiles - 1)),
            dma((count // block + 1, tiles - 1)),
            dma,
            dma((spans + 1, tiles - 1)),
            dma((spans + 1, tiles - 1)),
            dma((spans,)),
            dma((spans,)),
            dma((spans,)),
            dma((2,)),
            dma((n_one,)),
        ],
        compiler_params=pltpu.CompilerParams(
            collective_id=0, has_side_effects=True, vmem_limit_bytes=63 << 20
        ),
    )(
        raw_echo,
        phase_scaling,
        phase_range,
        phase_azimuth,
        left_table(rows, np.arange(q), m, -1),
        twist_table(4, m, extent, 1),
        right_table(lane, lane, LANES, -1),
        right_table(lane, lane, LANES, 1, 1.0 / ranges),
        np.stack([c, s]).astype(np.float32),
        left_table(rows, rows, m, 1, 1.0 / extent),
    )


def solution(mesh):
    return jax.shard_map(
        body,
        mesh=mesh,
        in_specs=(
            P(None, ("strip", "az", "tile"), None),
            P(None, "tile"),
            P("tile", None),
            P(None, "tile"),
        ),
        out_specs=P(None, ("strip", "az"), "tile"),
        check_vma=False,
    )
```
